512 devices in a mesh: row: 128 (over z, y, core), col: 4 (over x).
Axes of the slice: x: 4, y: 8, z: 8, core: 2. Of those that a mesh axis runs over, the one named last changes fastest.
Arguments:
- kernel_panel: float32 [65536, 512], P('row', 'col'), may hold values from -66 to 66, as said below
- kernel_slab: float32 [65536, 2048], P('row', 'col'), may hold values from -6 to 6
Outputs:
- factor_panel: float32 [65536, 512], P('row', 'col')
- schur_slab: float32 [65536, 2048], P('row', 'col')
The draws below stay inside these ranges and needn't reach their ends.
Inputs may be any that keep to these rules, and one draw needn't show every extreme that they name: `kernel_panel`: the first 512 rows form a symmetric positive definite matrix whose smallest eigenvalue is 0.5 or more.
All inputs are finite; a program needn't handle non-finite values.
Results may differ from the reference program's by a relative error of at most 0.00011.
Values sent between devices are 32-bit elements; how exact they have to be, the bound alone decides.
No kernel may reach another device: no remote copies, remote signals or barrier semaphores. Data moves between devices by JAX's collectives and lax.ppermute only.
A program may use at most 64 MiB of HBM per device.

```python
import jax
import jax.numpy as jnp
from jax import lax

PANEL = 512
ROWS_DEV = 512
ORDER = 65536
SLAB = 2048
N_ROW = 128


def draw_kernel_panel(key, part):
    key_gram = jax.random.fold_in(key, 11)
    key_rest = jax.random.fold_in(key, 12)
    source = jax.random.truncated_normal(key_gram, -4.0, 4.0, (PANEL, PANEL), jnp.float32)
    gram = jnp.dot(source, source.T, precision=lax.Precision.HIGHEST) / PANEL
    leading_block = 0.5 * (gram + gram.T) + 0.5 * jnp.eye(PANEL, dtype=jnp.float32)
    rest_rows = 0.25 * jax.random.truncated_normal(key_rest, -4.0, 4.0, (ORDER - PANEL, PANEL), jnp.float32)
    return jnp.concatenate([leading_block, rest_rows], axis=0)


def block_levels(stream_key, dims, shards, smallest, high):
    gain = 1.0
    for dim, blocks in shards:
        steps = jax.random.uniform(jax.random.fold_in(jax.random.fold_in(stream_key, 6), dim), (blocks,), jnp.float32, smallest / len(shards), high / len(shards))
        gain = gain * jnp.repeat(jnp.exp(steps), dims[dim] // blocks).reshape((-1,) + (1,) * (len(dims) - 1 - dim))
    return gain


def centred(rng, dims, width, reach, pieces=(), kind=jnp.bfloat16):
    values = width * jax.random.normal(rng, dims, jnp.float32)
    if pieces:
        values = values * block_levels(rng, dims, pieces, -0.22, 0.18)
    return jnp.clip(values, -reach, reach).astype(kind)


def setup_inputs(seed: int = 0) -> dict:
    keys = jax.random.split(jax.random.key(seed), 3)
    return {
        "kernel_panel": draw_kernel_panel(jax.random.fold_in(keys[2], 71), 0),
        "kernel_slab": centred(keys[1], (ORDER, SLAB), 1.0, 6.0, ((0, 128), (1, 4)), jnp.float32),
    }


def reference(kernel_panel, kernel_slab):
    leading_block = kernel_panel[:PANEL]
    leading_factor = jnp.linalg.cholesky(leading_block)
    lower_full = jax.scipy.linalg.solve_triangular(leading_factor, kernel_panel.T, lower=True).T
    row_ids = lax.iota(jnp.int32, ORDER)
    col_ids = lax.iota(jnp.int32, PANEL)
    lower_full = jnp.where(col_ids[None, :] <= row_ids[:, None], lower_full, jnp.zeros_like(lower_full))
    block_ids = lax.iota(jnp.int32, SLAB // ROWS_DEV)
    row_table = ((1 + block_ids % (N_ROW - 1)) * ROWS_DEV)[:, None] + lax.iota(jnp.int32, ROWS_DEV)[None, :]
    far_rows = jnp.take(lower_full, row_table.reshape(-1).astype(jnp.int32), axis=0)
    update = lax.dot_general(lower_full.astype(jnp.float32), far_rows.astype(jnp.float32), (((1,), (1,)), ((), ())), precision=lax.Precision.HIGHEST, preferred_element_type=jnp.float32)
    return (lower_full, kernel_slab - update)
```

```python
import jax
import jax.numpy as jnp
from jax import lax
from jax.experimental import pallas as pl
from jax.experimental.pallas import tpu as pltpu
from jax.sharding import Mesh
from jax.sharding import PartitionSpec as P

ROW = ("z", "y", "k")
PLANE = ("z", "y")
F32 = jnp.float32
BF16 = jnp.bfloat16
STRIP = 8
BLOCK = 128


def split3(x):
    high = x.astype(BF16).astype(F32)
    rest = x - high
    mid = rest.astype(BF16).astype(F32)
    return high, mid, rest - mid


def outer_update(left, right):
    l1, l2, l3 = split3(left)
    r1, r2, r3 = split3(right)
    lhs = jnp.concatenate([l1, l1, l2, l1, l3, l2], axis=0).astype(BF16)
    rhs = jnp.concatenate([r1, r2, r1, r3, r1, r2], axis=0).astype(BF16)
    return lax.dot_general(lhs, rhs, (((0,), (0,)), ((), ())), preferred_element_type=F32)


def mul_t(a, b):
    return lax.dot_general(
        a, b, (((1,), (1,)), ((), ())), precision=lax.Precision.HIGHEST, preferred_element_type=F32
    )


def factor_block(d):
    row = lax.broadcasted_iota(jnp.int32, (STRIP, BLOCK), 0)
    lane = lax.broadcasted_iota(jnp.int32, (STRIP, BLOCK), 1)
    lane_full = lax.broadcasted_iota(jnp.int32, (BLOCK, BLOCK), 1)
    for o in range(0, BLOCK, STRIP):
        s = d[o : o + STRIP, :]
        cols = [jnp.broadcast_to(s[:, o + m : o + m + 1], (STRIP, BLOCK)) for m in range(STRIP)]
        s = jnp.where((lane >= o) & (lane < o + STRIP), jnp.where(lane - o == row, 1.0, 0.0), s)
        for j in range(STRIP):
            scale = lax.rsqrt(jnp.broadcast_to(cols[j][j : j + 1, :], (STRIP, BLOCK)))
            lj = cols[j] * scale
            below = jnp.where(row > j, lj, 0.0)
            pivot = jnp.broadcast_to(s[j : j + 1, :], (STRIP, BLOCK)) * scale
            s = jnp.where(row == j, pivot, s - below * pivot)
            for m in range(j + 1, STRIP):
                cols[m] = cols[m] - below * jnp.broadcast_to(lj[m : m + 1, :], (STRIP, BLOCK))
        d[o : o + STRIP, :] = s
        n = o + STRIP
        if n < BLOCK:
            update = outer_update(jnp.where(lane >= n, s, 0.0), s)
            lf = lane_full[n:, :]
            d[n:, :] = jnp.where((lf >= o) & (lf < n), 0.0, d[n:, :]) - update[n:, :]


def kernel(idx, g, h, x0, x1, x2, x3, slab, factor, schur, a, far, x, d):
    core, col, row_start = idx[0], idx[1], idx[2]
    size = slab.shape[0]

    def unpack(low, high):
        for half, ref in ((0, low), (1, high)):
            for j in range(2):
                a[2 * half + j] = ref[:, j].reshape(size, BLOCK)
                far[2 * half + j] = ref[:, 2 + j].reshape(size, BLOCK)

    @pl.when(core == 0)
    def _():
        unpack(g, h)

    @pl.when(core != 0)
    def _():
        unpack(h, g)

    for s, ref in enumerate((x0, x1, x2, x3)):
        x[lax.rem(col - s + 4, 4)] = ref[...]

    blocks = size // BLOCK
    tri = lax.broadcasted_iota(jnp.int32, (BLOCK, BLOCK), 0) >= lax.broadcasted_iota(
        jnp.int32, (BLOCK, BLOCK), 1
    )
    for j in range(blocks):
        o = j * BLOCK
        n = o + BLOCK
        d[...] = a[j, o:n, :]
        factor_block(d)
        inverse = jnp.where(tri, d[...], 0.0)
        if j + 1 < blocks:
            below = mul_t(a[j, n:, :], inverse)
            for m in range(j + 1, blocks):
                lo = (m - j - 1) * BLOCK
                a[m, m * BLOCK :, :] = a[m, m * BLOCK :, :] - mul_t(below[lo:], below[lo : lo + BLOCK])
        for ref in (x, far):
            solved = mul_t(ref[j], inverse)
            ref[j] = solved
            for m in range(j + 1, blocks):
                lo = (m - j - 1) * BLOCK
                ref[m] = ref[m] - mul_t(solved, below[lo : lo + BLOCK])
    rows = row_start + lax.broadcasted_iota(jnp.int32, (size, BLOCK), 0)
    lanes = lax.broadcasted_iota(jnp.int32, (size, BLOCK), 1)
    total = slab[...]
    for j in range(blocks):
        x[j] = jnp.where(lanes + j * BLOCK <= rows, x[j], 0.0)
        total = total - mul_t(x[j], far[j])
    schur[...] = total
    factor[...] = x[col]


def run_kernel(idx, g, h, xs, slab):
    size = slab.shape[0]
    vmem = pl.BlockSpec(memory_space=pltpu.VMEM)
    return pl.pallas_call(
        kernel,
        out_shape=(
            jax.ShapeDtypeStruct((size, BLOCK), F32),
            jax.ShapeDtypeStruct((size, size), F32),
        ),
        in_specs=[pl.BlockSpec(memory_space=pltpu.SMEM)] + [vmem] * 7,
        out_specs=(vmem, vmem),
        scratch_shapes=[pltpu.VMEM((4, size, BLOCK), F32)] * 3 + [pltpu.VMEM((BLOCK, BLOCK), F32)],
        compiler_params=pltpu.CompilerParams(vmem_limit_bytes=24 << 20),
    )(idx, g, h, *xs, slab)


def ring(n, s):
    return [(i, (i + s) % n) for i in range(n)]


def plan(kernel_panel, kernel_slab):
    core, col = lax.axis_index("k"), lax.axis_index("x")
    row_start = lax.axis_index(ROW) * kernel_panel.shape[0]
    right = lax.ppermute(kernel_panel, "x", ring(4, 1))
    left = lax.ppermute(kernel_panel, "x", ring(4, 3))
    across = lax.ppermute(kernel_panel, "x", ring(4, 2))

    pieces = lax.all_to_all(kernel_panel.reshape(64, 8, BLOCK), PLANE, 0, 0, tiled=True)
    parcel = jnp.stack([jnp.stack([pieces[0], pieces[(1 + c) // 2]]) for c in range(4)])
    parcel = jnp.broadcast_to(parcel[None], (2, 4, 2, 8, BLOCK)).reshape(8, 2, 8, BLOCK)
    parcel = lax.all_to_all(parcel, ("k", "x"), 0, 0, tiled=True).reshape(2, 4, 2, 8, BLOCK)
    lead = lax.dynamic_slice_in_dim(parcel[0, :, 0], 2 * core, 2, 0)
    far = lax.dynamic_index_in_dim(parcel[:, :, 1], lax.rem(1 + col, 2), 0, keepdims=False)
    far = lax.dynamic_slice_in_dim(far, 2 * core, 2, 0)
    mine = jnp.concatenate([lead, far], axis=0)
    spread = jnp.broadcast_to(mine[None], (64, 4, 8, BLOCK))
    g = lax.all_to_all(spread, PLANE, 0, 0, tiled=True)
    h = lax.ppermute(g, "k", ring(2, 1))
    idx = jnp.stack([core, col, row_start]).astype(jnp.int32)
    return run_kernel(idx, g, h, (kernel_panel, right, across, left), kernel_slab)


def solution(mesh):
    torus = Mesh(mesh.devices.reshape(8, 8, 2, mesh.shape["col"]), ("z", "y", "k", "x"))
    spec = P(ROW, "x")
    return jax.shard_map(
        plan, mesh=torus, in_specs=(spec, spec), out_specs=(spec, spec), check_vma=False
    )
```

```python
import jax
import jax.numpy as jnp
from jax import lax
from jax.experimental import pallas as pl
from jax.experimental.pallas import tpu as pltpu
from jax.sharding import Mesh
from jax.sharding import PartitionSpec as P

ROW = ("z", "y", "k")
PLANE = ("z", "y")
F32 = jnp.float32
BF16 = jnp.bfloat16
STRIP = 8
BLOCK = 128
STRIPS = BLOCK // STRIP
AHEAD = 3


def split3(x):
    high = x.astype(BF16).astype(F32)
    rest = x - high
    mid = rest.astype(BF16).astype(F32)
    return high, mid, rest - mid


def outer_update(left, right):
    l1, l2, l3 = split3(left)
    r1, r2, r3 = split3(right)
    lhs = jnp.concatenate([l1, l1, l2, l1, l3, l2], axis=0).astype(BF16)
    rhs = jnp.concatenate([r1, r2, r1, r3, r1, r2], axis=0).astype(BF16)
    return lax.dot_general(lhs, rhs, (((0,), (0,)), ((), ())), preferred_element_type=F32)


def mul_t(a, b):
    return lax.dot_general(
        a, b, (((1,), (1,)), ((), ())), precision=lax.Precision.HIGHEST, preferred_element_type=F32
    )


def mul_t3(a, b):
    a1, b1 = a.astype(BF16), b.astype(BF16)
    a2, b2 = (a - a1.astype(F32)).astype(BF16), (b - b1.astype(F32)).astype(BF16)

    def dot(left, right):
        return lax.dot_general(left, right, (((1,), (1,)), ((), ())), preferred_element_type=F32)

    return dot(a1, b1) + (dot(a1, b2) + dot(a2, b1))


def over_lanes(x, lane):
    return jnp.broadcast_to(x[:, lane : lane + 1], (STRIP, BLOCK))


def over_rows(x, r):
    return jnp.broadcast_to(x[r : r + 1, :], (STRIP, BLOCK))


def factor_block(load, store):
    row = lax.broadcasted_iota(jnp.int32, (STRIP, BLOCK), 0)
    lane = lax.broadcasted_iota(jnp.int32, (STRIP, BLOCK), 1)
    rows = [load(t) for t in range(STRIPS)]
    spread = {}
    for b in range(STRIPS):
        o = b * STRIP
        window = range(b, min(b + AHEAD + 1, STRIPS))
        below = window[1:]
        inside = (lane >= o) & (lane < o + STRIP)
        now = {t: spread.get(t) or [over_lanes(rows[t], o + m) for m in range(STRIP)] for t in window}
        later = {t: [over_lanes(rows[t], o + STRIP + m) for m in range(STRIP)] for t in below}
        unit = jnp.where(lane - o == row, 1.0, 0.0)
        strip = {t: jnp.where(inside, unit if t == b else 0.0, rows[t]) for t in window}
        for j in range(STRIP):
            scale = lax.rsqrt(over_rows(now[b][j], j))
            column = now[b][j] * scale
            across = {m: over_rows(column, m) for m in range(j + 1, STRIP)}
            for m in across:
                now[b][m] = now[b][m] - column * across[m]
            pivot = over_rows(strip[b], j) * scale
            reduced = strip[b] - jnp.where(row > j, column, 0.0) * pivot
            strip[b] = jnp.where(row == j, pivot, reduced)
            across_next = None
            for t in below:
                column = now[t][j] * scale
                strip[t] = strip[t] - column * pivot
                for m in across:
                    now[t][m] = now[t][m] - column * across[m]
                if t == b + 1:
                    across_next = [over_rows(column, m) for m in range(STRIP)]
                for m in range(STRIP):
                    later[t][m] = later[t][m] - column * across_next[m]
        for t in window:
            rows[t] = strip[t]
        store(b, strip[b])
        spread = later
        n = b + AHEAD + 1
        if n < STRIPS:
            update = outer_update(jnp.where(lane >= n * STRIP, strip[b], 0.0), strip[b])
            for t in range(n, STRIPS):
                rows[t] = jnp.where(inside, 0.0, rows[t]) - update[t * STRIP : (t + 1) * STRIP]


def unpack(core, mine, other, out):
    size = out.shape[1]

    def place(low, high):
        for half, ref in ((0, low), (1, high)):
            for j in range(2):
                out[2 * half + j] = ref[:, j].reshape(size, BLOCK)

    @pl.when(core == 0)
    def _():
        place(mine, other)

    @pl.when(core != 0)
    def _():
        place(other, mine)


def place_of(row_block, col_block):
    return row_block * (row_block - 1) // 2 + col_block


def factor_kernel(idx, mine, other, inverse, lower, a, d):
    blocks = a.shape[0]
    unpack(idx[0], mine, other, a)
    tri = lax.broadcasted_iota(jnp.int32, (BLOCK, BLOCK), 0) >= lax.broadcasted_iota(
        jnp.int32, (BLOCK, BLOCK), 1
    )
    for j in range(blocks):
        o = j * BLOCK
        n = o + BLOCK

        def load(t, j=j, o=o):
            return a[j, o + t * STRIP : o + (t + 1) * STRIP, :]

        def store(t, value):
            d[t * STRIP : (t + 1) * STRIP, :] = value

        factor_block(load, store)
        inv = jnp.where(tri, d[...], 0.0)
        inverse[j] = inv
        if j + 1 < blocks:
            below = mul_t(a[j, n:, :], inv)
            for m in range(j + 1, blocks):
                lo = (m - j - 1) * BLOCK
                s = m * BLOCK
                lower[place_of(m, j)] = below[lo : lo + BLOCK]
                a[m, s:, :] = a[m, s:, :] - mul_t(below[lo:], below[lo : lo + BLOCK])


def solve(x, inverse, lower):
    blocks = x.shape[0]
    for j in range(blocks):
        solved = mul_t(x[j], inverse[j])
        x[j] = solved
        for m in range(j + 1, blocks):
            x[m] = x[m] - mul_t(solved, lower[place_of(m, j)])


def own_kernel(idx, own0, own1, own2, own3, inverse, lower, out, factor):
    col, row_start = idx[1], idx[2]
    blocks, size = out.shape[0], out.shape[1]
    for shift, ref in enumerate((own0, own1, own2, own3)):
        out[lax.rem(col - shift + blocks, blocks)] = ref[...]
    solve(out, inverse, lower)
    rows = row_start + lax.broadcasted_iota(jnp.int32, (size, BLOCK), 0)
    lanes = lax.broadcasted_iota(jnp.int32, (size, BLOCK), 1)
    for j in range(blocks):
        out[j] = jnp.where(lanes + j * BLOCK <= rows, out[j], 0.0)
    factor[...] = out[col]


def schur_kernel(idx, own, mine, other, inverse, lower, slab, schur, far):
    unpack(idx[0], mine, other, far)
    solve(far, inverse, lower)
    total = slab[...]
    for j in range(far.shape[0]):
        total = total - mul_t3(own[j], far[j])
    schur[...] = total


def call(body, outs, flops, scratch, *args):
    vmem = pl.BlockSpec(memory_space=pltpu.VMEM)
    bytes_accessed = sum(4 * a.size for a in args) + sum(4 * o.size for o in outs)
    return pl.pallas_call(
        body,
        out_shape=outs,
        in_specs=[pl.BlockSpec(memory_space=pltpu.SMEM)] + [vmem] * (len(args) - 1),
        out_specs=tuple(vmem for _ in outs),
        scratch_shapes=[pltpu.VMEM(s, F32) for s in scratch],
        compiler_params=pltpu.CompilerParams(vmem_limit_bytes=16 << 20),
        cost_estimate=pl.CostEstimate(
            flops=flops, bytes_accessed=bytes_accessed, transcendentals=0
        ),
    )(*args)


def plan(kernel_panel, kernel_slab):
    size = kernel_panel.shape[0]
    core, col = lax.axis_index("k"), lax.axis_index("x")
    row_start = lax.axis_index(ROW) * size
    idx = jnp.stack([core, col, row_start]).astype(jnp.int32)

    pieces = lax.all_to_all(kernel_panel.reshape(64, 8, BLOCK), PLANE, 0, 0, tiled=True)
    parcel = jnp.stack([jnp.stack([pieces[0], pieces[(1 + c) // 2]]) for c in range(4)])
    parcel = jnp.broadcast_to(parcel[None], (2, 4, 2, 8, BLOCK)).reshape(8, 2, 8, BLOCK)
    parcel = lax.all_to_all(parcel, ("k", "x"), 0, 0, tiled=True).reshape(2, 4, 2, 8, BLOCK)
    lead = lax.dynamic_slice_in_dim(parcel[0, :, 0], 2 * core, 2, 0)
    far = lax.dynamic_index_in_dim(parcel[:, :, 1], lax.rem(1 + col, 2), 0, keepdims=False)
    far = lax.dynamic_slice_in_dim(far, 2 * core, 2, 0)

    def spread(piece):
        copies = jnp.broadcast_to(piece[None], (64, 2, 8, BLOCK))
        return lax.all_to_all(copies, PLANE, 0, 0, tiled=True)

    lead = spread(lead)
    lead_other = lax.ppermute(lead, "k", [(0, 1), (1, 0)])
    far = spread(far)
    own = [kernel_panel]
    for shift in (1, 2, 3):
        own.append(lax.ppermute(kernel_panel, "x", [(i, (i + shift) % 4) for i in range(4)]))
    blocks = jax.ShapeDtypeStruct((4, size, BLOCK), F32)
    inverse, lower = call(
        factor_kernel,
        (
            jax.ShapeDtypeStruct((4, BLOCK, BLOCK), F32),
            jax.ShapeDtypeStruct((6, BLOCK, BLOCK), F32),
        ),
        2 * 10**10,
        [(4, size, BLOCK), (BLOCK, BLOCK)],
        idx,
        lead,
        lead_other,
    )
    far_other = lax.ppermute(far, "k", [(0, 1), (1, 0)])
    own, factor = call(
        own_kernel,
        (blocks, jax.ShapeDtypeStruct((size, BLOCK), F32)),
        2 * 10**9,
        [],
        idx,
        *own,
        inverse,
        lower,
    )
    (schur,) = call(
        schur_kernel,
        (jax.ShapeDtypeStruct((size, size), F32),),
        4 * 10**9,
        [(4, size, BLOCK)],
        idx,
        own,
        far,
        far_other,
        inverse,
        lower,
        kernel_slab,
    )
    return factor, schur


def solution(mesh):
    torus = Mesh(mesh.devices.reshape(8, 8, 2, mesh.shape["col"]), ("z", "y", "k", "x"))
    spec = P(ROW, "x")
    return jax.shard_map(
        plan, mesh=torus, in_specs=(spec, spec), out_specs=(spec, spec), check_vma=False
    )
```

```python
import jax
import jax.numpy as jnp
from jax import lax
from jax.experimental import pallas as pl
from jax.experimental.pallas import tpu as pltpu
from jax.sharding import Mesh
from jax.sharding import PartitionSpec as P

ROW = ("z", "y", "k")
PLANE = ("z", "y")
F32 = jnp.float32
BF16 = jnp.bfloat16
STRIP = 8
BLOCK = 128
STRIPS = BLOCK // STRIP
AHEAD = 3


def split3(x):
    high = x.astype(BF16).astype(F32)
    rest = x - high
    mid = rest.astype(BF16).astype(F32)
    return high, mid, rest - mid


def outer_update(left, right):
    l1, l2, l3 = split3(left)
    r1, r2, r3 = split3(right)
    lhs = jnp.concatenate([l1, l1, l2, l1, l3, l2], axis=0).astype(BF16)
    rhs = jnp.concatenate([r1, r2, r1, r3, r1, r2], axis=0).astype(BF16)
    return lax.dot_general(lhs, rhs, (((0,), (0,)), ((), ())), preferred_element_type=F32)


def mul_t(a, b):
    return lax.dot_general(
        a, b, (((1,), (1,)), ((), ())), precision=lax.Precision.HIGHEST, preferred_element_type=F32
    )


def mul(a, b):
    return jnp.dot(a, b, precision=lax.Precision.HIGHEST, preferred_element_type=F32)


def mul_t3(a, b):
    a1, b1 = a.astype(BF16), b.astype(BF16)
    a2, b2 = (a - a1.astype(F32)).astype(BF16), (b - b1.astype(F32)).astype(BF16)

    def dot(left, right):
        return lax.dot_general(left, right, (((1,), (1,)), ((), ())), preferred_element_type=F32)

    return dot(a1, b1) + (dot(a1, b2) + dot(a2, b1))


def over_lanes(x, lane):
    return jnp.broadcast_to(x[:, lane : lane + 1], (STRIP, BLOCK))


def over_rows(x, r):
    return jnp.broadcast_to(x[r : r + 1, :], (STRIP, BLOCK))


def factor_block(load, store):
    row = lax.broadcasted_iota(jnp.int32, (STRIP, BLOCK), 0)
    lane = lax.broadcasted_iota(jnp.int32, (STRIP, BLOCK), 1)
    rows = [load(t) for t in range(STRIPS)]
    spread = {}
    for b in range(STRIPS):
        o = b * STRIP
        window = range(b, min(b + AHEAD + 1, STRIPS))
        below = window[1:]
        inside = (lane >= o) & (lane < o + STRIP)
        now = {t: spread.get(t) or [over_lanes(rows[t], o + m) for m in range(STRIP)] for t in window}
        later = {t: [over_lanes(rows[t], o + STRIP + m) for m in range(STRIP)] for t in below}
        unit = jnp.where(lane - o == row, 1.0, 0.0)
        strip = {t: jnp.where(inside, unit if t == b else 0.0, rows[t]) for t in window}
        for j in range(STRIP):
            scale = lax.rsqrt(over_rows(now[b][j], j))
            column = now[b][j] * scale
            across = {m: over_rows(column, m) for m in range(j + 1, STRIP)}
            for m in across:
                now[b][m] = now[b][m] - column * across[m]
            pivot = over_rows(strip[b], j) * scale
            reduced = strip[b] - jnp.where(row > j, column, 0.0) * pivot
            strip[b] = jnp.where(row == j, pivot, reduced)
            across_next = None
            for t in below:
                column = now[t][j] * scale
                strip[t] = strip[t] - column * pivot
                for m in across:
                    now[t][m] = now[t][m] - column * across[m]
                if t == b + 1:
                    across_next = [over_rows(column, m) for m in range(STRIP)]
                for m in range(STRIP):
                    later[t][m] = later[t][m] - column * across_next[m]
        for t in window:
            rows[t] = strip[t]
        store(b, strip[b])
        spread = later
        n = b + AHEAD + 1
        if n < STRIPS:
            update = outer_update(jnp.where(lane >= n * STRIP, strip[b], 0.0), strip[b])
            for t in range(n, STRIPS):
                rows[t] = jnp.where(inside, 0.0, rows[t]) - update[t * STRIP : (t + 1) * STRIP]


def unpack(core, mine, other, out):
    size = out.shape[0]

    def place(low, high):
        for half, ref in ((0, low), (1, high)):
            for j in range(2):
                o = (2 * half + j) * BLOCK
                out[:, o : o + BLOCK] = ref[:, j].reshape(size, BLOCK)

    @pl.when(core == 0)
    def _():
        place(mine, other)

    @pl.when(core != 0)
    def _():
        place(other, mine)


def factor_kernel(idx, mine, other, top, bottom, a, inverse, d):
    size = a.shape[0]
    half = size // 2
    unpack(idx[0], mine, other, a)
    tri = lax.broadcasted_iota(jnp.int32, (BLOCK, BLOCK), 0) >= lax.broadcasted_iota(
        jnp.int32, (BLOCK, BLOCK), 1
    )
    for o in range(0, size, BLOCK):
        n = o + BLOCK

        def load(t, o=o, n=n):
            return a[o + t * STRIP : o + (t + 1) * STRIP, o:n]

        def store(t, value):
            d[t * STRIP : (t + 1) * STRIP, :] = value

        factor_block(load, store)
        inv = jnp.where(tri, d[...], 0.0)
        inverse[o:n, o:n] = inv
        if n < size:
            inverse[o:n, n:] = jnp.zeros((BLOCK, size - n), F32)
            below = mul_t(a[n:, o:n], inv)
            a[n:, o:n] = below
            for m in range(n, size, BLOCK):
                lo = m - n
                e = m + BLOCK
                a[m:, m:e] = a[m:, m:e] - mul_t(below[lo:], below[lo : lo + BLOCK])
        if o > 0:
            inverse[o:n, :o] = 0.0 - mul(inv, mul(a[o:n, :o], inverse[:o, :o]))
    top[...] = inverse[:half, :half]
    bottom[...] = inverse[half:, :]


def solve(x, top, bottom):
    half = x.shape[1] // 2
    return mul_t(x[:, :half], top[...]), mul_t(x[...], bottom[...])


def own_kernel(idx, own0, own1, own2, own3, top, bottom, out, factor, x):
    col, row_start = idx[1], idx[2]
    size = x.shape[0]
    half = size // 2

    def lanes_of(block):
        return pl.ds(pl.multiple_of(block * BLOCK, BLOCK), BLOCK)

    for shift, ref in enumerate((own0, own1, own2, own3)):
        x[:, lanes_of(lax.rem(col - shift + 4, 4))] = ref[...]
    rows = row_start + lax.broadcasted_iota(jnp.int32, (size, half), 0)
    lanes = lax.broadcasted_iota(jnp.int32, (size, half), 1)
    for part, solved in enumerate(solve(x, top, bottom)):
        o = part * half
        out[:, o : o + half] = jnp.where(lanes + o <= rows, solved, 0.0)
    factor[...] = out[:, lanes_of(col)]


def schur_kernel(idx, own, mine, other, top, bottom, slab, schur, far):
    half = far.shape[0] // 2
    unpack(idx[0], mine, other, far)
    low, high = solve(far, top, bottom)
    schur[...] = slab[...] - (mul_t3(own[:, :half], low) + mul_t3(own[:, half:], high))


def call(body, outs, flops, scratch, *args):
    vmem = pl.BlockSpec(memory_space=pltpu.VMEM)
    bytes_accessed = sum(4 * a.size for a in args) + sum(4 * o.size for o in outs)
    return pl.pallas_call(
        body,
        out_shape=outs,
        in_specs=[pl.BlockSpec(memory_space=pltpu.SMEM)] + [vmem] * (len(args) - 1),
        out_specs=tuple(vmem for _ in outs),
        scratch_shapes=[pltpu.VMEM(s, F32) for s in scratch],
        compiler_params=pltpu.CompilerParams(vmem_limit_bytes=16 << 20),
        cost_estimate=pl.CostEstimate(
            flops=flops, bytes_accessed=bytes_accessed, transcendentals=0
        ),
    )(*args)


def plan(kernel_panel, kernel_slab):
    size = kernel_panel.shape[0]
    core, col = lax.axis_index("k"), lax.axis_index("x")
    row_start = lax.axis_index(ROW) * size
    idx = jnp.stack([core, col, row_start]).astype(jnp.int32)

    pieces = lax.all_to_all(kernel_panel.reshape(64, 8, BLOCK), PLANE, 0, 0, tiled=True)
    parcel = jnp.stack([jnp.stack([pieces[0], pieces[(1 + c) // 2]]) for c in range(4)])
    parcel = jnp.broadcast_to(parcel[None], (2, 4, 2, 8, BLOCK)).reshape(8, 2, 8, BLOCK)
    parcel = lax.all_to_all(parcel, ("k", "x"), 0, 0, tiled=True).reshape(2, 4, 2, 8, BLOCK)
    lead = lax.dynamic_slice_in_dim(parcel[0, :, 0], 2 * core, 2, 0)
    far = lax.dynamic_index_in_dim(parcel[:, :, 1], lax.rem(1 + col, 2), 0, keepdims=False)
    far = lax.dynamic_slice_in_dim(far, 2 * core, 2, 0)

    def spread(piece):
        copies = jnp.broadcast_to(piece[None], (64, 2, 8, BLOCK))
        return lax.all_to_all(copies, PLANE, 0, 0, tiled=True)

    lead = spread(lead)
    lead_other = lax.ppermute(lead, "k", [(0, 1), (1, 0)])
    far = spread(far)
    own = [kernel_panel]
    for shift in (1, 2, 3):
        own.append(lax.ppermute(kernel_panel, "x", [(i, (i + shift) % 4) for i in range(4)]))
    square = jax.ShapeDtypeStruct((size, size), F32)
    inverse = call(
        factor_kernel,
        (
            jax.ShapeDtypeStruct((size // 2, size // 2), F32),
            jax.ShapeDtypeStruct((size // 2, size), F32),
        ),
        2 * 10**10,
        [(size, size), (size, size), (BLOCK, BLOCK)],
        idx,
        lead,
        lead_other,
    )
    far_other = lax.ppermute(far, "k", [(0, 1), (1, 0)])
    own, factor = call(
        own_kernel,
        (square, jax.ShapeDtypeStruct((size, BLOCK), F32)),
        2 * 10**9,
        [(size, size)],
        idx,
        *own,
        *inverse,
    )
    (schur,) = call(
        schur_kernel,
        (square,),
        4 * 10**9,
        [(size, size)],
        idx,
        own,
        far,
        far_other,
        *inverse,
        kernel_slab,
    )
    return factor, schur


def solution(mesh):
    torus = Mesh(mesh.devices.reshape(8, 8, 2, mesh.shape["col"]), ("z", "y", "k", "x"))
    spec = P(ROW, "x")
    return jax.shard_map(
        plan, mesh=torus, in_specs=(spec, spec), out_specs=(spec, spec), check_vma=False
    )
```

```python
import jax
import jax.numpy as jnp
from jax import lax
from jax.experimental import pallas as pl
from jax.experimental.pallas import tpu as pltpu
from jax.sharding import Mesh
from jax.sharding import PartitionSpec as P

ROW = ("z", "y", "k")
PLANE = ("z", "y")
F32 = jnp.float32
BF16 = jnp.bfloat16
STRIP = 8
BLOCK = 128
STRIPS = BLOCK // STRIP
AHEAD = 3
CHUNKS = 4


def split3(x):
    high = x.astype(BF16).astype(F32)
    rest = x - high
    mid = rest.astype(BF16).astype(F32)
    return high, mid, rest - mid


def outer_update(left, right):
    l1, l2, l3 = split3(left)
    r1, r2, r3 = split3(right)
    lhs = jnp.concatenate([l1, l1, l2, l1, l3, l2], axis=0).astype(BF16)
    rhs = jnp.concatenate([r1, r2, r1, r3, r1, r2], axis=0).astype(BF16)
    return lax.dot_general(lhs, rhs, (((0,), (0,)), ((), ())), preferred_element_type=F32)


def mul_t(a, b):
    return lax.dot_general(
        a, b, (((1,), (1,)), ((), ())), precision=lax.Precision.HIGHEST, preferred_element_type=F32
    )


def mul(a, b):
    return jnp.dot(a, b, precision=lax.Precision.HIGHEST, preferred_element_type=F32)


def mul_t3(a, b):
    a1, b1 = a.astype(BF16), b.astype(BF16)
    a2, b2 = (a - a1.astype(F32)).astype(BF16), (b - b1.astype(F32)).astype(BF16)

    def dot(left, right):
        return lax.dot_general(left, right, (((1,), (1,)), ((), ())), preferred_element_type=F32)

    return dot(a1, b1) + (dot(a1, b2) + dot(a2, b1))


def over_lanes(x, lane):
    return jnp.broadcast_to(x[:, lane : lane + 1], (STRIP, BLOCK))


def over_rows(x, r):
    return jnp.broadcast_to(x[r : r + 1, :], (STRIP, BLOCK))


def factor_block(load, store, background=()):
    background = list(background)
    every = -(-STRIPS // max(len(background), 1))
    row = lax.broadcasted_iota(jnp.int32, (STRIP, BLOCK), 0)
    lane = lax.broadcasted_iota(jnp.int32, (STRIP, BLOCK), 1)
    rows = [load(t) for t in range(STRIPS)]
    spread = {}
    for b in range(STRIPS):
        if background and b % every == 0:
            background.pop(0)()
        o = b * STRIP
        window = range(b, min(b + AHEAD + 1, STRIPS))
        below = window[1:]
        inside = (lane >= o) & (lane < o + STRIP)
        now = {t: spread.get(t) or [over_lanes(rows[t], o + m) for m in range(STRIP)] for t in window}
        later = {t: [over_lanes(rows[t], o + STRIP + m) for m in range(STRIP)] for t in below}
        unit = jnp.where(lane - o == row, 1.0, 0.0)
        strip = {t: jnp.where(inside, unit if t == b else 0.0, rows[t]) for t in window}
        for j in range(STRIP):
            scale = lax.rsqrt(over_rows(now[b][j], j))
            column = now[b][j] * scale
            across = {m: over_rows(column, m) for m in range(j + 1, STRIP)}
            for m in across:
                now[b][m] = now[b][m] - column * across[m]
            pivot = over_rows(strip[b], j) * scale
            reduced = strip[b] - jnp.where(row > j, column, 0.0) * pivot
            strip[b] = jnp.where(row == j, pivot, reduced)
            across_next = None
            for t in below:
                column = now[t][j] * scale
                strip[t] = strip[t] - column * pivot
                for m in across:
                    now[t][m] = now[t][m] - column * across[m]
                if t == b + 1:
                    across_next = [over_rows(column, m) for m in range(STRIP)]
                for m in range(STRIP):
                    later[t][m] = later[t][m] - column * across_next[m]
        for t in window:
            rows[t] = strip[t]
        store(b, strip[b])
        spread = later
        n = b + AHEAD + 1
        if n < STRIPS:
            update = outer_update(jnp.where(lane >= n * STRIP, strip[b], 0.0), strip[b])
            for t in range(n, STRIPS):
                rows[t] = jnp.where(inside, 0.0, rows[t]) - update[t * STRIP : (t + 1) * STRIP]


def unpack(core, mine, other, item, out, start):
    size = mine.shape[0] * mine.shape[2]

    def place(low, high):
        for half, ref in ((0, low), (1, high)):
            for j in range(2):
                o = (2 * half + j) * BLOCK
                out[start : start + size, o : o + BLOCK] = ref[:, item + j].reshape(size, BLOCK)

    @pl.when(core == 0)
    def _():
        place(mine, other)

    @pl.when(core != 0)
    def _():
        place(other, mine)


def kernel(idx, mine, other, own0, own1, own2, own3, slab, factor, schur, a, inverse, d, x, f):
    core, col, row_start = idx[0], idx[1], idx[2]
    size = a.shape[0]
    half = size // 2
    unpack(core, mine, other, 0, a, 0)
    unpack(core, mine, other, 2, x, size)

    def lanes_of(block):
        return pl.ds(pl.multiple_of(block * BLOCK, BLOCK), BLOCK)

    for shift, ref in enumerate((own0, own1, own2, own3)):
        x[:size, lanes_of(lax.rem(col - shift + 4, 4))] = ref[...]
    tri = lax.broadcasted_iota(jnp.int32, (BLOCK, BLOCK), 0) >= lax.broadcasted_iota(
        jnp.int32, (BLOCK, BLOCK), 1
    )

    def solve(first, last, chunks):
        rows = 2 * size // chunks

        def chunk(r):
            f[r : r + rows, first:last] = mul_t(x[r : r + rows, :last], inverse[first:last, :last])

        return [lambda r=r: chunk(r) for r in range(0, 2 * size, rows)]

    for o in range(0, size, BLOCK):
        n = o + BLOCK

        def load(t, o=o, n=n):
            return a[o + t * STRIP : o + (t + 1) * STRIP, o:n]

        def store(t, value):
            d[t * STRIP : (t + 1) * STRIP, :] = value

        if o == half:
            background = solve(0, half, CHUNKS)
        elif o == half + BLOCK:
            background = solve(half, o, CHUNKS)
        else:
            background = ()
        factor_block(load, store, background)
        inv = jnp.where(tri, d[...], 0.0)
        inverse[o:n, o:n] = inv
        if n < size:
            inverse[o:n, n:] = jnp.zeros((BLOCK, size - n), F32)
            below = mul_t(a[n:, o:n], inv)
            a[n:, o:n] = below
            for m in range(n, size, BLOCK):
                lo = m - n
                e = m + BLOCK
                a[m:, m:e] = a[m:, m:e] - mul_t(below[lo:], below[lo : lo + BLOCK])
        if o > 0:
            inverse[o:n, :o] = 0.0 - mul(inv, mul(a[o:n, :o], inverse[:o, :o]))
    solve(size - BLOCK, size, 1)[0]()
    rows = row_start + lax.broadcasted_iota(jnp.int32, (size, size), 0)
    lanes = lax.broadcasted_iota(jnp.int32, (size, size), 1)
    f[:size, :] = jnp.where(lanes <= rows, f[:size, :], 0.0)
    factor[...] = f[:size, lanes_of(col)]
    schur[...] = slab[...] - mul_t3(f[:size, :], f[size:, :])


def run_kernel(idx, mine, other, own0, own1, own2, own3, slab):
    size = slab.shape[0]
    vmem = pl.BlockSpec(memory_space=pltpu.VMEM)
    return pl.pallas_call(
        kernel,
        name="factor",
        out_shape=(
            jax.ShapeDtypeStruct((size, BLOCK), F32),
            jax.ShapeDtypeStruct((size, size), F32),
        ),
        in_specs=[pl.BlockSpec(memory_space=pltpu.SMEM)] + [vmem] * 7,
        out_specs=(vmem, vmem),
        scratch_shapes=[
            pltpu.VMEM((size, size), F32),
            pltpu.VMEM((size, size), F32),
            pltpu.VMEM((BLOCK, BLOCK), F32),
            pltpu.VMEM((2 * size, size), F32),
            pltpu.VMEM((2 * size, size), F32),
        ],
        compiler_params=pltpu.CompilerParams(vmem_limit_bytes=16 << 20),
    )(idx, mine, other, own0, own1, own2, own3, slab)


def plan(kernel_panel, kernel_slab):
    size = kernel_panel.shape[0]
    core, col = lax.axis_index("k"), lax.axis_index("x")
    row_start = lax.axis_index(ROW) * size
    idx = jnp.stack([core, col, row_start]).astype(jnp.int32)

    pieces = lax.all_to_all(kernel_panel.reshape(64, 8, BLOCK), PLANE, 0, 0, tiled=True)
    parcel = jnp.stack([jnp.stack([pieces[0], pieces[(1 + c) // 2]]) for c in range(4)])
    parcel = jnp.broadcast_to(parcel[None], (2, 4, 2, 8, BLOCK)).reshape(8, 2, 8, BLOCK)
    parcel = lax.all_to_all(parcel, ("k", "x"), 0, 0, tiled=True).reshape(2, 4, 2, 8, BLOCK)
    lead = lax.dynamic_slice_in_dim(parcel[0, :, 0], 2 * core, 2, 0)
    far = lax.dynamic_index_in_dim(parcel[:, :, 1], lax.rem(1 + col, 2), 0, keepdims=False)
    far = lax.dynamic_slice_in_dim(far, 2 * core, 2, 0)

    copies = jnp.broadcast_to(jnp.concatenate([lead, far])[None], (64, 4, 8, BLOCK))
    mine = lax.all_to_all(copies, PLANE, 0, 0, tiled=True)
    other = lax.ppermute(mine, "k", [(0, 1), (1, 0)])
    own = [kernel_panel]
    for shift in (1, 2, 3):
        own.append(lax.ppermute(kernel_panel, "x", [(i, (i + shift) % 4) for i in range(4)]))
    return run_kernel(idx, mine, other, *own, kernel_slab)


def solution(mesh):
    torus = Mesh(mesh.devices.reshape(8, 8, 2, mesh.shape["col"]), ("z", "y", "k", "x"))
    spec = P(ROW, "x")
    return jax.shard_map(
        plan, mesh=torus, in_specs=(spec, spec), out_specs=(spec, spec), check_vma=False
    )
```

```python
import jax
import jax.numpy as jnp
from jax import lax
from jax.experimental import pallas as pl
from jax.experimental.pallas import tpu as pltpu
from jax.sharding import Mesh
from jax.sharding import PartitionSpec as P

ROW = ("z", "y", "k")
PLANE = ("y", "z")
F32 = jnp.float32
BF16 = jnp.bfloat16
STRIP = 8
BLOCK = 128
STRIPS = BLOCK // STRIP
AHEAD = 3
CHUNKS = 4


def split3(x):
    high = x.astype(BF16).astype(F32)
    rest = x - high
    mid = rest.astype(BF16).astype(F32)
    return high, mid, rest - mid


def outer_update(left, right):
    l1, l2, l3 = split3(left)
    r1, r2, r3 = split3(right)
    lhs = jnp.concatenate([l1, l1, l2, l1, l3, l2], axis=0).astype(BF16)
    rhs = jnp.concatenate([r1, r2, r1, r3, r1, r2], axis=0).astype(BF16)
    return lax.dot_general(lhs, rhs, (((0,), (0,)), ((), ())), preferred_element_type=F32)


def mul_t(a, b):
    return lax.dot_general(
        a, b, (((1,), (1,)), ((), ())), precision=lax.Precision.HIGHEST, preferred_element_type=F32
    )


def mul(a, b):
    return jnp.dot(a, b, precision=lax.Precision.HIGHEST, preferred_element_type=F32)


def dot_t(a, b):
    return lax.dot_general(a, b, (((1,), (1,)), ((), ())), preferred_element_type=F32)


def over_lanes(x, lane):
    return jnp.broadcast_to(x[:, lane : lane + 1], (STRIP, BLOCK))


def over_rows(x, r):
    return jnp.broadcast_to(x[r : r + 1, :], (STRIP, BLOCK))


def factor_block(load, store, background=()):
    background = list(background)
    every = max(STRIPS // max(len(background), 1), 1)
    row = lax.broadcasted_iota(jnp.int32, (STRIP, BLOCK), 0)
    lane = lax.broadcasted_iota(jnp.int32, (STRIP, BLOCK), 1)
    rows = [load(t) for t in range(STRIPS)]
    spread = {}
    for b in range(STRIPS):
        if background and b % every == 0:
            background.pop(0)()
        o = b * STRIP
        window = range(b, min(b + AHEAD + 1, STRIPS))
        below = window[1:]
        inside = (lane >= o) & (lane < o + STRIP)
        now = {t: spread.get(t) or [over_lanes(rows[t], o + m) for m in range(STRIP)] for t in window}
        later = {t: [over_lanes(rows[t], o + STRIP + m) for m in range(STRIP)] for t in below}
        unit = jnp.where(lane - o == row, 1.0, 0.0)
        strip = {t: jnp.where(inside, unit if t == b else 0.0, rows[t]) for t in window}
        for j in range(STRIP):
            scale = lax.rsqrt(over_rows(now[b][j], j))
            column = now[b][j] * scale
            across = {m: over_rows(column, m) for m in range(j + 1, STRIP)}
            for m in across:
                now[b][m] = now[b][m] - column * across[m]
            pivot = over_rows(strip[b], j) * scale
            reduced = strip[b] - jnp.where(row > j, column, 0.0) * pivot
            strip[b] = jnp.where(row == j, pivot, reduced)
            across_next = None
            for t in below:
                column = now[t][j] * scale
                strip[t] = strip[t] - column * pivot
                for m in across:
                    now[t][m] = now[t][m] - column * across[m]
                if t == b + 1:
                    across_next = [over_rows(column, m) for m in range(STRIP)]
                for m in range(STRIP):
                    later[t][m] = later[t][m] - column * across_next[m]
        for t in window:
            rows[t] = strip[t]
        store(b, strip[b])
        spread = later
        n = b + AHEAD + 1
        if n < STRIPS:
            update = outer_update(jnp.where(lane >= n * STRIP, strip[b], 0.0), strip[b])
            for t in range(n, STRIPS):
                rows[t] = jnp.where(inside, 0.0, rows[t]) - update[t * STRIP : (t + 1) * STRIP]
    for work in background:
        work()


def kernel(
    idx, mine, other, own0, own1, own2, own3, slab, factor, schur, a, inverse, d, x, f, high, rest
):
    core, col, row_start = idx[0], idx[1], idx[2]
    size = a.shape[0]
    half = size // 2
    last = size - BLOCK

    def received(item, block):
        place = 2 * item + block % 2
        near, away = mine[:, place], other[:, place]
        return jnp.where(core == block // 2, near, away).reshape(size, BLOCK)

    def lanes_of(block):
        return pl.ds(pl.multiple_of(block * BLOCK, BLOCK), BLOCK)

    def take_far(block):
        x[size:, block * BLOCK : (block + 1) * BLOCK] = received(1, block)

    def take_own(shift, ref):
        x[:size, lanes_of(lax.rem(col - shift + 4, 4))] = ref[...]

    def solve(first, end, chunks):
        rows = 2 * size // chunks

        def chunk(r):
            value = mul_t(x[r : r + rows, :end], inverse[first:end, :end])
            if r < size:
                row = row_start + r + lax.broadcasted_iota(jnp.int32, (rows, end - first), 0)
                lane = first + lax.broadcasted_iota(jnp.int32, (rows, end - first), 1)
                value = jnp.where(lane <= row, value, 0.0)
                f[r : r + rows, first:end] = value
            top = value.astype(BF16)
            high[r : r + rows, first:end] = top
            rest[r : r + rows, first:end] = (value - top.astype(F32)).astype(BF16)

        return [lambda r=r: chunk(r) for r in range(0, 2 * size, rows)]

    def update(base, first, end, chunks):
        rows = size // chunks

        def chunk(r):
            h, t = high[r : r + rows, first:end], rest[r : r + rows, first:end]
            far_h, far_t = high[size:, first:end], rest[size:, first:end]
            product = dot_t(h, far_h) + (dot_t(h, far_t) + dot_t(t, far_h))
            schur[r : r + rows, :] = base[r : r + rows, :] - product

        return [lambda r=r: chunk(r) for r in range(0, size, rows)]

    def finish(o):
        n = o + BLOCK
        e = n + BLOCK

        def panel():
            if e < size:
                below = mul_t(a[e:, o:n], inverse[o:n, o:n])
                a[e:, o:n] = below
                a[e:, n:e] = a[e:, n:e] - mul_t(below, a[n:e, o:n])

        def trailing(m):
            a[m:, m : m + BLOCK] = a[m:, m : m + BLOCK] - mul_t(a[m:, o:n], a[m : m + BLOCK, o:n])

        def invert():
            if o > 0:
                left = mul(a[o:n, :o], inverse[:o, :o])
                inverse[o:n, :o] = 0.0 - mul(inverse[o:n, o:n], left)

        tail = [lambda m=m: trailing(m) for m in range(e, size, BLOCK)]
        return [panel] + tail + [invert]

    for block in range(4):
        a[:, block * BLOCK : (block + 1) * BLOCK] = received(0, block)
    inverse[:half, BLOCK:last] = jnp.zeros((half, last - BLOCK), F32)
    tri = lax.broadcasted_iota(jnp.int32, (BLOCK, BLOCK), 0) >= lax.broadcasted_iota(
        jnp.int32, (BLOCK, BLOCK), 1
    )
    background = [lambda block=block: take_far(block) for block in range(4)] + [
        lambda shift=shift, ref=ref: take_own(shift, ref)
        for shift, ref in enumerate((own0, own1, own2, own3))
    ]
    for o in range(0, size, BLOCK):
        n = o + BLOCK

        def load(t, o=o, n=n):
            return a[o + t * STRIP : o + (t + 1) * STRIP, o:n]

        def store(t, value):
            d[t * STRIP : (t + 1) * STRIP, :] = value

        factor_block(load, store, background)
        inv = jnp.where(tri, d[...], 0.0)
        inverse[o:n, o:n] = inv
        if n < size:
            e = n + BLOCK
            beside = mul_t(a[n:e, o:n], inv)
            a[n:e, o:n] = beside
            a[n:e, n:e] = a[n:e, n:e] - mul_t(beside, beside)
            background = finish(o)
        if n == half:
            background = background + solve(0, half, CHUNKS)
        elif n == last:
            background = background + solve(half, last, CHUNKS) + update(slab, 0, half, 2)
    finish(last)[-1]()
    for chunk in solve(last, size, 2) + update(schur, half, size, 1):
        chunk()
    factor[...] = f[:, lanes_of(col)]


def run_kernel(idx, mine, other, own0, own1, own2, own3, slab):
    size = slab.shape[0]
    vmem = pl.BlockSpec(memory_space=pltpu.VMEM)
    return pl.pallas_call(
        kernel,
        name="factor",
        out_shape=(
            jax.ShapeDtypeStruct((size, BLOCK), F32),
            jax.ShapeDtypeStruct((size, size), F32),
        ),
        in_specs=[pl.BlockSpec(memory_space=pltpu.SMEM)] + [vmem] * 7,
        out_specs=(vmem, vmem),
        scratch_shapes=[
            pltpu.VMEM((size, size), F32),
            pltpu.VMEM((size, size), F32),
            pltpu.VMEM((BLOCK, BLOCK), F32),
            pltpu.VMEM((2 * size, size), F32),
            pltpu.VMEM((size, size), F32),
            pltpu.VMEM((2 * size, size), BF16),
            pltpu.VMEM((2 * size, size), BF16),
        ],
        compiler_params=pltpu.CompilerParams(vmem_limit_bytes=16 << 20),
    )(idx, mine, other, own0, own1, own2, own3, slab)


def plan(kernel_panel, kernel_slab):
    size = kernel_panel.shape[0]
    core, col = lax.axis_index("k"), lax.axis_index("x")
    row_start = lax.axis_index(ROW) * size
    idx = jnp.stack([core, col, row_start]).astype(jnp.int32)

    pieces = lax.all_to_all(kernel_panel.reshape(64, 8, BLOCK), PLANE, 0, 0, tiled=True)
    parcel = jnp.stack([jnp.stack([pieces[0], pieces[8 * ((1 + c) // 2)]]) for c in range(4)])
    parcel = jnp.broadcast_to(parcel[None], (2, 4, 2, 8, BLOCK)).reshape(8, 2, 8, BLOCK)
    parcel = lax.all_to_all(parcel, ("k", "x"), 0, 0, tiled=True).reshape(2, 4, 2, 8, BLOCK)
    lead = lax.dynamic_slice_in_dim(parcel[0, :, 0], 2 * core, 2, 0)
    far = lax.dynamic_index_in_dim(parcel[:, :, 1], lax.rem(1 + col, 2), 0, keepdims=False)
    far = lax.dynamic_slice_in_dim(far, 2 * core, 2, 0)

    copies = jnp.broadcast_to(jnp.concatenate([lead, far])[None], (64, 4, 8, BLOCK))
    mine = lax.all_to_all(copies, PLANE, 0, 0, tiled=True)
    other = lax.ppermute(mine, "k", [(0, 1), (1, 0)])
    own = [kernel_panel]
    for shift in (1, 2, 3):
        own.append(lax.ppermute(kernel_panel, "x", [(i, (i + shift) % 4) for i in range(4)]))
    return run_kernel(idx, mine, other, *own, kernel_slab)


def solution(mesh):
    torus = Mesh(mesh.devices.reshape(8, 8, 2, mesh.shape["col"]), ("z", "y", "k", "x"))
    spec = P(ROW, "x")
    return jax.shard_map(
        plan, mesh=torus, in_specs=(spec, spec), out_specs=(spec, spec), check_vma=False
    )
```
